128 devices in a mesh: dp: 16 (over y_hi, z, core), shard: 8 (over x, y_lo).
Axes of the slice: x: 4, y: 4 (y_hi: 2, y_lo: 2; y = y_hi * 2 + y_lo), z: 4, core: 2. Of those that a mesh axis runs over, the one named last changes fastest.
Arguments:
- queries: float32 [65536, 256], P(('dp', 'shard'))
- items: float32 [163840, 256], P('shard')
- positive: int32 [65536], P(('dp', 'shard')), may hold values from 0 to 163839
- tile_ids: int32 [128, 8, 3], P(('dp', 'shard')), may hold values from 0 to 39, as said below
- counts: int32 [128, 8], P(('dp', 'shard')), may hold values from 1 to 3, as said below
Outputs:
- loss: float32 [65536], P(('dp', 'shard'))
- query_grad: float32 [65536, 256], P(('dp', 'shard'))
- item_grad: float32 [163840, 256], P(('shard', 'dp'))
The draws below stay inside these ranges and needn't reach their ends.
Inputs may be any that keep to these rules, and one draw needn't show every extreme that they name: `tile_ids`: within one block and shard the 3 entries are distinct; only the first counts of them are visited. `counts`: every block visits exactly 3 tiles on at least one shard.
All inputs are finite; a program needn't handle non-finite values.
Results may differ from the reference program's by a relative error of at most 0.0003.
Values sent between devices are 32-bit elements; how exact they have to be, the bound alone decides.
A program may use at most 192 MiB of HBM per device.

```python
import jax
import jax.numpy as jnp
from jax import lax

D = 256
TILE = 512
TILES_DEV = 40
QDEV = 512
KMAX = 3
BLOCKS = 128
QUERIES = 65536
ITEMS = 163840
N_SHARD = 8


def shared_items(key):
    return jax.random.normal(jax.random.fold_in(key, 5), (ITEMS, D), jnp.float32)


def shared_positive(key):
    return jax.random.randint(jax.random.fold_in(key, 11), (QUERIES,), 0, ITEMS, dtype=jnp.int32)


def shared_tile_ids(key):
    scores = jax.random.randint(jax.random.fold_in(key, 21), (BLOCKS, N_SHARD, TILES_DEV), 0, 1048576, dtype=jnp.int32)
    scores = scores * TILES_DEV + jnp.arange(TILES_DEV, dtype=jnp.int32)
    order = jnp.argsort(scores, axis=-1, stable=True)
    return order[:, :, :KMAX].astype(jnp.int32)


def draw_items(key, part):
    return shared_items(key)


def draw_positive(key, part):
    return shared_positive(key)


def draw_tile_ids(key, part):
    return shared_tile_ids(key)


def draw_queries(key, part):
    base = jax.random.normal(jax.random.fold_in(key, 3), (QUERIES, D), jnp.float32) * 0.0625
    table = shared_items(key)
    pos_id = shared_positive(key)
    row_ids = jnp.arange(QUERIES, dtype=jnp.int32)
    first_tile = shared_tile_ids(key)[row_ids // QDEV, 0, 0]
    cand_id = first_tile * TILE + row_ids % TILE
    other_id = first_tile * TILE + (row_ids + 1) % TILE
    cand_id = jnp.where(cand_id == pos_id, other_id, cand_id)
    pos_vec = table[pos_id]
    cand_vec = table[cand_id]
    pp = jnp.sum(pos_vec * pos_vec, axis=1)
    pc = jnp.sum(pos_vec * cand_vec, axis=1)
    cc = jnp.sum(cand_vec * cand_vec, axis=1)
    level = jax.random.uniform(jax.random.fold_in(key, 4), (QUERIES,), jnp.float32, 110.0, 300.0)
    gap = jax.random.uniform(jax.random.fold_in(key, 7), (QUERIES,), jnp.float32, 1.0, 3.0)
    second = level - gap
    det = pp * cc - pc * pc
    coef_p = (level * cc - second * pc) / det
    coef_c = (second * pp - level * pc) / det
    aligned = coef_p[:, None] * pos_vec + coef_c[:, None] * cand_vec
    picked = (row_ids % 64 == 0)[:, None]
    return jnp.where(picked, aligned, base)


def draw_counts(key, part):
    heavy = jax.random.randint(jax.random.fold_in(key, 31), (BLOCKS, 1), 0, N_SHARD, dtype=jnp.int32)
    lighter = jax.random.randint(jax.random.fold_in(key, 32), (BLOCKS, N_SHARD), 1, KMAX, dtype=jnp.int32)
    return jnp.where(jnp.arange(N_SHARD, dtype=jnp.int32)[None, :] == heavy, KMAX, lighter).astype(jnp.int32)


def setup_inputs(seed: int = 0) -> dict:
    seeds = jax.random.split(jax.random.key(seed), 6)
    return {
        "queries": draw_queries(jax.random.fold_in(seeds[5], 71), 0),
        "items": draw_items(jax.random.fold_in(seeds[5], 71), 0),
        "positive": draw_positive(jax.random.fold_in(seeds[5], 71), 0),
        "tile_ids": draw_tile_ids(jax.random.fold_in(seeds[5], 71), 0),
        "counts": draw_counts(jax.random.fold_in(seeds[5], 71), 0),
    }


very_low = -1.0e30


def reference(queries, items, positive, tile_ids, counts):
    blocks = QUERIES // QDEV
    local_rows = TILES_DEV * TILE
    query_blocks = queries.reshape(blocks, QDEV, D)
    pos_blocks = positive.reshape(blocks, QDEV)
    high = lax.Precision.HIGHEST

    def one_block(grads, xs):
        qblk, pblk, ids, cnt = xs
        starts = jnp.arange(N_SHARD, dtype=jnp.int32)[:, None] * local_rows + ids * TILE
        row_index = (starts[:, :, None] + jnp.arange(TILE, dtype=jnp.int32)[None, None, :]).reshape(-1)
        live = jnp.arange(KMAX, dtype=jnp.int32)[None, :] < cnt[:, None]
        live = jnp.broadcast_to(live[:, :, None], (N_SHARD, KMAX, TILE)).reshape(-1)
        cand = items[row_index]
        logits = jnp.dot(qblk, cand.T, precision=high, preferred_element_type=jnp.float32)
        logits = jnp.where(live[None, :], logits, very_low)
        chosen = items[pblk]
        plogit = jnp.sum(qblk * chosen, axis=1)
        top = jnp.maximum(jnp.max(logits, axis=1), plogit)
        total = jnp.sum(jnp.where(live[None, :], jnp.exp(logits - top[:, None]), 0.0), axis=1) + jnp.exp(plogit - top)
        lse = top + jnp.log(total)
        loss = lse - plogit
        prob = jnp.where(live[None, :], jnp.exp(logits - lse[:, None]), 0.0)
        weight = jnp.exp(plogit - lse) - 1.0
        dq = jnp.dot(prob, cand, precision=high, preferred_element_type=jnp.float32) + weight[:, None] * chosen
        grads = grads.at[row_index].add(jnp.dot(prob.T, qblk, precision=high, preferred_element_type=jnp.float32))
        grads = grads.at[pblk].add(weight[:, None] * qblk)
        return grads, (loss, dq)

    start = jnp.zeros((ITEMS, D), jnp.float32)
    grads, (loss, dq) = lax.scan(one_block, start, (query_blocks, pos_blocks, tile_ids, counts))
    return loss.reshape(QUERIES), dq.reshape(QUERIES, D), grads
```

```python
import jax
import jax.numpy as jnp
from jax import lax
from jax.sharding import PartitionSpec as P

TILE = 512


very_low = -1e30


def joined(part, axis, combine):
    gathered = jax.tree.map(lambda a: lax.all_gather(a, axis), part)

    def take(source):
        return jax.tree.map(lambda a: lax.dynamic_index_in_dim(a, source, 0, False), gathered)

    return lax.fori_loop(
        1, lax.axis_size(axis), lambda source, state: combine(state, take(source)), take(0)
    )


def positive_row(qblk, pblk, items, shard_at):
    local_rows = items.shape[0]
    offset = pblk - shard_at * local_rows
    inside = (offset >= 0) & (offset < local_rows)
    safe = jnp.clip(offset, 0, local_rows - 1)
    target = jnp.where(inside, offset, local_rows)
    chosen = jnp.take(items, safe, axis=0)
    logit = jnp.where(inside, jnp.sum(qblk * chosen, axis=1), 0.0)
    return (inside, target, chosen, logit)


def tile_logits(qblk, items, tile):
    block = lax.dynamic_slice_in_dim(items, tile * TILE, TILE, 0)
    logits = jnp.einsum(
        "qd,td->qt",
        qblk,
        block,
        precision=lax.Precision.HIGHEST,
        preferred_element_type=jnp.float32,
    )
    return (logits, block)


def block_stats(qblk, pblk, idrow, count, items, shard_at):
    rows = qblk.shape[0]

    def visit(step, carry):
        top, total = carry
        logits, block = tile_logits(qblk, items, idrow[step])
        new_top = jnp.maximum(top, jnp.max(logits, axis=1))
        total = total * jnp.exp(top - new_top) + jnp.sum(jnp.exp(logits - new_top[:, None]), axis=1)
        return (new_top, total)

    start = (jnp.full((rows,), very_low, jnp.float32), jnp.zeros((rows,), jnp.float32))
    top, total = lax.fori_loop(0, count, visit, start)
    inside, target, chosen, logit = positive_row(qblk, pblk, items, shard_at)
    new_top = jnp.maximum(top, jnp.where(inside, logit, very_low))
    total = total * jnp.exp(top - new_top) + jnp.where(inside, jnp.exp(logit - new_top), 0.0)
    return ((new_top, total, logit), (inside, target, chosen))


def block_grads(qblk, idrow, count, lse, items, d_local, inside, chosen, plogit):
    high = lax.Precision.HIGHEST

    def visit(step, carry):
        dq, grads = carry
        tile = idrow[step]
        logits, block = tile_logits(qblk, items, tile)
        prob = jnp.exp(logits - lse[:, None])
        dq = dq + jnp.dot(prob, block, precision=high, preferred_element_type=jnp.float32)
        update = jnp.einsum(
            "qt,qd->td", prob, qblk, precision=high, preferred_element_type=jnp.float32
        )
        current = lax.dynamic_slice_in_dim(grads, tile * TILE, TILE, 0)
        grads = lax.dynamic_update_slice_in_dim(grads, current + update, tile * TILE, 0)
        return (dq, grads)

    dq, d_local = lax.fori_loop(0, count, visit, (jnp.zeros(qblk.shape, jnp.float32), d_local))
    weight = jnp.where(inside, jnp.exp(plogit - lse) - 1.0, 0.0)
    dq = dq + weight[:, None] * chosen
    return (dq, d_local, weight[:, None] * qblk)


def combine_stats(first, second):
    top = jnp.maximum(first[0], second[0])
    total = first[1] * jnp.exp(first[0] - top) + second[1] * jnp.exp(second[0] - top)
    return (top, total, first[2] + second[2])


def gather_packed(queries, positive, tile_ids, counts):
    rows, width = queries.shape
    n_shard = lax.axis_size("shard")
    pos_rows = rows // width
    ints = jnp.concatenate([tile_ids.reshape(-1), counts.reshape(-1)]).astype(jnp.float32)
    extra = jnp.zeros((8, width), jnp.float32)
    extra = extra.at[:pos_rows].set(positive.astype(jnp.float32).reshape(pos_rows, width))
    extra = extra.at[pos_rows, : ints.shape[0]].set(ints)
    packed = jnp.concatenate([queries, extra], axis=0)
    seen = lax.all_gather(packed, "shard")
    seen_q = seen[:, :rows]
    seen_pos = seen[:, rows : rows + pos_rows].reshape(n_shard, rows).astype(jnp.int32)
    n_ids = tile_ids.size
    flat = seen[:, rows + pos_rows].astype(jnp.int32)
    seen_ids = flat[:, :n_ids].reshape((n_shard,) + tile_ids.shape[1:])
    seen_cnt = flat[:, n_ids : n_ids + counts.size].reshape((n_shard,) + counts.shape[1:])
    return seen_q, seen_pos, seen_ids, seen_cnt


def local(queries, items, positive, tile_ids, counts):
    shard_at = lax.axis_index("shard")
    n_shard = lax.axis_size("shard")
    rows = queries.shape[0]
    width = queries.shape[1]
    seen_q, seen_pos, seen_ids, seen_cnt = gather_packed(queries, positive, tile_ids, counts)
    idrows = jnp.take(seen_ids, shard_at, axis=1)
    seen_counts = jnp.take(seen_cnt, shard_at, axis=1)

    def stats_of(xs):
        return block_stats(xs[0], xs[1], xs[2], xs[3], items, shard_at)

    (tops, totals, plogs), (insides, targets, chosens) = lax.map(
        stats_of, (seen_q, seen_pos, idrows, seen_counts)
    )
    local_plogs = plogs
    stacked = lax.all_gather(jnp.stack([tops, totals, plogs]), "shard")
    tops, totals, plogs = lax.fori_loop(
        1,
        n_shard,
        lambda source, state: combine_stats(state, tuple(stacked[source])),
        tuple(stacked[0]),
    )
    lse = tops + jnp.log(totals)
    loss = jnp.take(lse, shard_at, axis=0) - jnp.take(plogs, shard_at, axis=0)
    d_local = jnp.zeros(items.shape, jnp.float32)

    def grads_of(grads, xs):
        dq, grads, update = block_grads(
            xs[0], xs[1], xs[2], xs[3], items, grads, xs[4], xs[5], xs[6]
        )
        return (grads, (dq, update))

    d_local, (dq_parts, updates) = lax.scan(
        grads_of, d_local, (seen_q, idrows, seen_counts, lse, insides, chosens, local_plogs)
    )
    d_local = d_local.at[targets.reshape(-1)].add(updates.reshape(-1, width), mode="drop")
    query_grad = lax.psum_scatter(dq_parts, "shard", scatter_dimension=0, tiled=True).reshape(
        rows, width
    )
    item_grad = lax.psum_scatter(d_local, "dp", scatter_dimension=0, tiled=True)
    return (loss, query_grad, item_grad)


def solution(mesh):
    placed = (
        P(("dp", "shard"), None),
        P("shard", None),
        P(("dp", "shard")),
        P(("dp", "shard"), None, None),
        P(("dp", "shard"), None),
    )
    return jax.shard_map(
        local,
        mesh=mesh,
        in_specs=placed,
        out_specs=(P(("dp", "shard")), P(("dp", "shard"), None), P(("shard", "dp"), None)),
        check_vma=False,
    )
```

```python
import functools

import jax
import jax.numpy as jnp
from jax import lax
from jax.experimental import pallas as pl
from jax.experimental.pallas import tpu as pltpu
from jax.sharding import PartitionSpec as P

TILE = 512
KMAX = 3

very_low = -1e30
BF = jnp.bfloat16
F32 = jnp.float32


def split(x):
    hi = x.astype(BF)
    return hi, (x - hi.astype(F32)).astype(BF)


def mm(a, b, ca, cb):
    return lax.dot_general(a, b, (((ca,), (cb,)), ((), ())), preferred_element_type=F32)


def mm3(ah, al, bh, bl, ca, cb):
    return mm(ah, bh, ca, cb) + mm(ah, bl, ca, cb) + mm(al, bh, ca, cb)


def stats_kernel(ids_ref, cnt_ref, q_ref, t_ref, m_out, l_out, dq_out, qh_s, ql_s, m_s, l_s, dq_s):
    j = pl.program_id(0)
    k = pl.program_id(1)

    @pl.when(k == 0)
    def _():
        qh, ql = split(q_ref[0])
        qh_s[...] = qh
        ql_s[...] = ql
        m_s[...] = jnp.full(m_s.shape, very_low, F32)
        l_s[...] = jnp.zeros(l_s.shape, F32)
        dq_s[...] = jnp.zeros(dq_s.shape, F32)

    @pl.when(k < cnt_ref[j])
    def _():
        th, tl = split(t_ref[...])
        logits = mm3(qh_s[...], ql_s[...], th, tl, 1, 1)
        m_old = m_s[...]
        m_new = jnp.maximum(m_old, jnp.max(logits, axis=1, keepdims=True))
        alpha = jnp.exp(m_old - m_new)
        prob = jnp.exp(logits - m_new)
        l_s[...] = alpha * l_s[...] + jnp.sum(prob, axis=1, keepdims=True)
        ph, plo = split(prob)
        dq_s[...] = alpha * dq_s[...] + mm3(ph, plo, th, tl, 1, 0)
        m_s[...] = m_new

    @pl.when(k == KMAX - 1)
    def _():
        m_out[0] = m_s[...]
        l_out[0] = l_s[...]
        dq_out[0] = dq_s[...]


def block_stats(seen_q, items, ids_flat, cnt):
    nb, rows, width = seen_q.shape

    def tile_map(j, k, ids, cnt):
        return (ids[j * KMAX + jnp.minimum(k, cnt[j] - 1)], 0)

    return pl.pallas_call(
        stats_kernel,
        out_shape=(
            jax.ShapeDtypeStruct((nb, rows, 1), F32),
            jax.ShapeDtypeStruct((nb, rows, 1), F32),
            jax.ShapeDtypeStruct((nb, rows, width), F32),
        ),
        grid_spec=pltpu.PrefetchScalarGridSpec(
            num_scalar_prefetch=2,
            grid=(nb, KMAX),
            in_specs=[
                pl.BlockSpec((1, rows, width), lambda j, k, ids, cnt: (j, 0, 0)),
                pl.BlockSpec((TILE, width), tile_map),
            ],
            out_specs=[
                pl.BlockSpec((1, rows, 1), lambda j, k, ids, cnt: (j, 0, 0)),
                pl.BlockSpec((1, rows, 1), lambda j, k, ids, cnt: (j, 0, 0)),
                pl.BlockSpec((1, rows, width), lambda j, k, ids, cnt: (j, 0, 0)),
            ],
            scratch_shapes=[
                pltpu.VMEM((rows, width), BF),
                pltpu.VMEM((rows, width), BF),
                pltpu.VMEM((rows, 1), F32),
                pltpu.VMEM((rows, 1), F32),
                pltpu.VMEM((rows, width), F32),
            ],
        ),
        compiler_params=pltpu.CompilerParams(dimension_semantics=("arbitrary", "arbitrary")),
        cost_estimate=pl.CostEstimate(
            flops=nb * KMAX * 6 * 2 * rows * TILE * width,
            transcendentals=nb * KMAX * rows * TILE,
            bytes_accessed=nb * (KMAX + 2) * rows * width * 4,
        ),
    )(ids_flat, cnt, seen_q, items)


def grads_kernel(ids_ref, cnt_ref, acc_ref, t_ref, q_ref, lse_ref, out_ref):
    t = pl.program_id(0)
    th, tl = split(t_ref[...])
    out_ref[...] = acc_ref[...]
    nb = q_ref.shape[0]

    def visit(v, carry):
        j = v // KMAX
        k = v % KMAX

        @pl.when((k < cnt_ref[j]) & (ids_ref[v] == t))
        def _():
            qh, ql = split(q_ref[j])
            logits_t = mm3(th, tl, qh, ql, 1, 1)
            prob_t = jnp.exp(logits_t - lse_ref[j])
            ph, plo = split(prob_t)
            out_ref[...] += mm3(ph, plo, qh, ql, 1, 0)

        return carry

    lax.fori_loop(0, nb * KMAX, visit, 0)


def tile_grads(acc, items, seen_q, lse, ids_flat, cnt):
    n_rows, width = items.shape
    nb, rows, _ = seen_q.shape
    n_tiles = n_rows // TILE
    return pl.pallas_call(
        grads_kernel,
        out_shape=jax.ShapeDtypeStruct((n_rows, width), F32),
        grid_spec=pltpu.PrefetchScalarGridSpec(
            num_scalar_prefetch=2,
            grid=(n_tiles,),
            in_specs=[
                pl.BlockSpec((TILE, width), lambda t, ids, cnt: (t, 0)),
                pl.BlockSpec((TILE, width), lambda t, ids, cnt: (t, 0)),
                pl.BlockSpec((nb, rows, width), lambda t, ids, cnt: (0, 0, 0)),
                pl.BlockSpec((nb, 1, rows), lambda t, ids, cnt: (0, 0, 0)),
            ],
            out_specs=pl.BlockSpec((TILE, width), lambda t, ids, cnt: (t, 0)),
        ),
        input_output_aliases={2: 0},
        compiler_params=pltpu.CompilerParams(dimension_semantics=("arbitrary",)),
        cost_estimate=pl.CostEstimate(
            flops=nb * KMAX * 6 * 2 * rows * TILE * width // 2,
            transcendentals=nb * KMAX * rows * TILE // 2,
            bytes_accessed=3 * n_rows * width * 4 + nb * rows * width * 4,
        ),
    )(ids_flat, cnt, acc, items, seen_q, lse)


def positive_row(qblk, pblk, items, shard_at):
    local_rows = items.shape[0]
    offset = pblk - shard_at * local_rows
    inside = (offset >= 0) & (offset < local_rows)
    safe = jnp.clip(offset, 0, local_rows - 1)
    target = jnp.where(inside, offset, local_rows)
    chosen = jnp.take(items, safe, axis=0)
    logit = jnp.where(inside, jnp.sum(qblk * chosen, axis=1), 0.0)
    return (inside, target, chosen, logit)


def gather_packed(queries, positive, tile_ids, counts):
    rows, width = queries.shape
    n_shard = lax.axis_size("shard")
    pos_rows = rows // width
    ints = jnp.concatenate([tile_ids.reshape(-1), counts.reshape(-1)]).astype(jnp.float32)
    extra = jnp.zeros((8, width), jnp.float32)
    extra = extra.at[:pos_rows].set(positive.astype(jnp.float32).reshape(pos_rows, width))
    extra = extra.at[pos_rows, : ints.shape[0]].set(ints)
    packed = jnp.concatenate([queries, extra], axis=0)
    seen = lax.all_gather(packed, "shard")
    seen_q = seen[:, :rows]
    seen_pos = seen[:, rows : rows + pos_rows].reshape(n_shard, rows).astype(jnp.int32)
    n_ids = tile_ids.size
    flat = seen[:, rows + pos_rows].astype(jnp.int32)
    seen_ids = flat[:, :n_ids].reshape((n_shard,) + tile_ids.shape[1:])
    seen_cnt = flat[:, n_ids : n_ids + counts.size].reshape((n_shard,) + counts.shape[1:])
    return seen_q, seen_pos, seen_ids, seen_cnt


def local(queries, items, positive, tile_ids, counts):
    shard_at = lax.axis_index("shard")
    n_shard = lax.axis_size("shard")
    rows = queries.shape[0]
    width = queries.shape[1]
    seen_q, seen_pos, seen_ids, seen_cnt = gather_packed(queries, positive, tile_ids, counts)
    idrows = jnp.take(seen_ids, shard_at, axis=1)
    ids_flat = idrows.reshape(-1)
    cnt = jnp.take(seen_cnt, shard_at, axis=1)

    m_loc, l_loc, dq_u = block_stats(seen_q, items, ids_flat, cnt)
    m_loc = m_loc.reshape(n_shard, rows)
    l_loc = l_loc.reshape(n_shard, rows)

    inside, target, chosen, plog = positive_row(
        seen_q.reshape(-1, width), seen_pos.reshape(-1), items, shard_at
    )
    plog = plog.reshape(n_shard, rows)
    inside = inside.reshape(n_shard, rows)

    stacked = lax.all_gather(jnp.stack([m_loc, l_loc, plog]), "shard")
    tops, totals, plogs = stacked[:, 0], stacked[:, 1], stacked[:, 2]
    plogit = jnp.sum(plogs, axis=0)
    top = jnp.maximum(jnp.max(tops, axis=0), plogit)
    total = jnp.sum(totals * jnp.exp(tops - top[None]), axis=0) + jnp.exp(plogit - top)
    lse = top + jnp.log(total)
    loss = jnp.take(lse, shard_at, axis=0) - jnp.take(plogit, shard_at, axis=0)

    scale = jnp.exp(m_loc - lse)
    weight = jnp.where(inside, jnp.exp(plogit - lse) - 1.0, 0.0)
    dq_parts = scale[:, :, None] * dq_u + weight[:, :, None] * chosen.reshape(n_shard, rows, width)
    query_grad = lax.psum_scatter(dq_parts, "shard", scatter_dimension=0, tiled=True).reshape(
        rows, width
    )

    updates = weight.reshape(-1)[:, None] * seen_q.reshape(-1, width)
    d_local = jnp.zeros(items.shape, F32).at[target].add(updates, mode="drop")
    d_local = tile_grads(d_local, items, seen_q, lse.reshape(n_shard, 1, rows), ids_flat, cnt)
    item_grad = lax.psum_scatter(d_local, "dp", scatter_dimension=0, tiled=True)
    return (loss, query_grad, item_grad)


def solution(mesh):
    placed = (
        P(("dp", "shard"), None),
        P("shard", None),
        P(("dp", "shard")),
        P(("dp", "shard"), None, None),
        P(("dp", "shard"), None),
    )
    return jax.shard_map(
        local,
        mesh=mesh,
        in_specs=placed,
        out_specs=(P(("dp", "shard")), P(("dp", "shard"), None), P(("shard", "dp"), None)),
        check_vma=False,
    )
```
